32 devices in a mesh: groups: 2 (over y), rows: 4 (over z), section: 2 (over x), feat: 2 (over core).
Axes of the slice: x: 2, y: 2, z: 4, core: 2. Of those that a mesh axis runs over, the one named last changes fastest.
Arguments:
- test_rows: bfloat16 [3, 256, 8, 512], P(None, ('groups', 'rows'), 'feat'), parts along dimension 1, may hold values from -6 to 6
- train_cache: bfloat16 [2, 2, 32, 8, 512], P('section', None, ('groups', 'rows'), 'feat'), parts along dimension 2, may hold values from -6 to 6
- pattern: int32 [8, 8], replicated, may hold values 0 or 1
- feat_qkv: bfloat16 [2, 512, 1536], P('section'), may hold values from -0.25 to 0.25
- feat_out: bfloat16 [2, 512, 512], P('section'), may hold values from -0.25 to 0.25
- item_query: bfloat16 [2, 512, 512], P('section'), may hold values from -0.25 to 0.25
- item_out: bfloat16 [2, 512, 512], P('section'), may hold values from -0.25 to 0.25
- gains: float32 [2, 2, 512], P('section'), may hold values from 0.5 to 1.5
Outputs:
- hidden: bfloat16 [2, 3, 256, 8, 512], P('section', None, ('groups', 'rows'), 'feat'), parts along dimension 2
The draws below stay inside these ranges and needn't reach their ends.
There are 2 independent parts, one for each index of `groups`. The reference program is written for one: setup_inputs(seed, part) draws one part's arguments, and reference() takes and returns one part's arrays. A program takes and returns all parts, laid end to end along the dimension named above; an argument that names none is the same for every part. Nothing has to cross between parts.
All inputs are finite; a program needn't handle non-finite values.
Results may differ from the reference program's by a relative error of at most 0.02.
Values may be sent and summed in bfloat16 or wider, within the bound.
No kernel may reach another device: no remote copies, remote signals or barrier semaphores. Data moves between devices by JAX's collectives and lax.ppermute only.
A program may use at most 64 MiB of HBM per device.

```python
import jax
import jax.numpy as jnp
from jax import lax

D = 512
HEADS = 8
MICRO = 3
LAYERS = 2
G = 8
TEST_ROWS = 128
TRAIN = 16


def with_ends(values, rng, least, high):
    longest = values.shape.index(max(values.shape))
    spots = []
    for shift in (0, 1):
        where = [jax.random.randint(jax.random.fold_in(rng, axis), (), 0, length) for axis, length in enumerate(values.shape)]
        where[longest] = (where[longest] + shift) % values.shape[longest]
        spots.append(tuple(where))
    return values.at[spots[0]].set(least).at[spots[1]].set(high)


def levels(key, shape, split, smallest, largest):
    level, own = 1.0, jax.random.fold_in(key, 6)
    for axis_at, parts in split:
        draws = jnp.exp(jax.random.uniform(jax.random.fold_in(own, axis_at), (parts,), jnp.float32, smallest / len(split), largest / len(split)))
        level = level * jnp.repeat(draws, shape[axis_at] // parts).reshape([-1 if axis == axis_at else 1 for axis in range(len(shape))])
    return level


def normal_values(own_key, shape, deviation, reach, cuts=(), kind=jnp.bfloat16):
    entries = deviation * jax.random.normal(own_key, shape, jnp.float32)
    if cuts:
        entries = entries * levels(own_key, shape, cuts, -0.22, 0.18)
    return jnp.clip(entries, -reach, reach).astype(kind)


def setup_inputs(seed: int = 0, part: int = 0) -> dict:
    splits = jax.random.split(jax.random.key(seed), 9)
    part_splits = jax.random.split(jax.random.fold_in(splits[8], part), 9)
    return {
        "test_rows": normal_values(part_splits[0], (MICRO, TEST_ROWS, G, D), 1.0, 6.0, ((1, 4), (2, 2))),
        "train_cache": normal_values(part_splits[1], (LAYERS, 2, TRAIN, G, D), 1.0, 6.0, ((0, 2), (2, 4), (3, 2))),
        "pattern": with_ends((jax.random.randint(splits[2], (G, G), 0, 2) < 1).astype(jnp.int32), jax.random.fold_in(splits[2], 1), 0, 1),
        "feat_qkv": normal_values(splits[3], (LAYERS, D, 3 * D), D ** -0.5, 0.25, ((0, 2),)),
        "feat_out": normal_values(splits[4], (LAYERS, D, D), D ** -0.5, 0.25, ((0, 2),)),
        "item_query": normal_values(splits[5], (LAYERS, D, D), D ** -0.5, 0.25, ((0, 2),)),
        "item_out": normal_values(splits[6], (LAYERS, D, D), D ** -0.5, 0.25, ((0, 2),)),
        "gains": jnp.clip(1.0 + 0.1 * jax.random.normal(splits[7], (LAYERS, 2, D), jnp.float32), 0.5, 1.5),
    }


HIGH = lax.Precision.HIGHEST

def normed(x, gain):
    mean_sq = lax.optimization_barrier(jnp.mean(x * x, axis=-1, keepdims=True))
    return x * lax.rsqrt(mean_sq + 1e-06) * gain

def one_layer(h, allowed, wqkv, wout, wquery, witem, gain_pair, cache):
    rows_n, groups, width = h.shape
    heads = HEADS
    head_dim = width // heads
    scale = 1.0 / head_dim ** 0.5
    a = normed(h, gain_pair[0]).astype(jnp.bfloat16).reshape(rows_n * groups, width)
    qkv = jnp.dot(a, wqkv, preferred_element_type=jnp.float32).astype(jnp.bfloat16)
    qkv = qkv.reshape(rows_n, groups, 3, heads, head_dim).astype(jnp.float32)
    query, keys, values = (qkv[:, :, 0], qkv[:, :, 1], qkv[:, :, 2])
    scores = jnp.einsum('rihd,rjhd->rhij', query, keys, precision=HIGH) * scale
    scores = jnp.where(allowed[None, None], scores, -1e+30)
    weights = jax.nn.softmax(scores, axis=-1).astype(jnp.bfloat16).astype(jnp.float32)
    mixed = jnp.einsum('rhij,rjhd->rihd', weights, values, precision=HIGH).astype(jnp.bfloat16)
    h1 = h + jnp.dot(mixed.reshape(rows_n * groups, width), wout, preferred_element_type=jnp.float32).reshape(rows_n, groups, width)
    b = normed(h1, gain_pair[1]).astype(jnp.bfloat16).reshape(rows_n * groups, width)
    item_q = jnp.dot(b, wquery, preferred_element_type=jnp.float32).astype(jnp.bfloat16)
    item_q = item_q.reshape(rows_n, groups, heads, head_dim).astype(jnp.float32)
    train_n = cache.shape[1]
    train_k = cache[0].astype(jnp.float32).reshape(train_n, groups, heads, head_dim)
    train_v = cache[1].astype(jnp.float32).reshape(train_n, groups, heads, head_dim)
    item_s = jnp.einsum('rghd,nghd->rghn', item_q, train_k, precision=HIGH) * scale
    probs = jax.nn.softmax(item_s, axis=-1)
    item_mix = jnp.einsum('rghn,nghd->rghd', probs, train_v, precision=HIGH).astype(jnp.bfloat16)
    item_term = jnp.dot(item_mix.reshape(rows_n * groups, width), witem, preferred_element_type=jnp.float32)
    return (h1 + item_term.reshape(rows_n, groups, width)).astype(jnp.bfloat16)

def reference(test_rows, train_cache, pattern, feat_qkv, feat_out, item_query, item_out, gains):
    groups = pattern.shape[0]
    allowed = (pattern != 0) | jnp.eye(groups, dtype=bool)
    per_layer = []
    states = [test_rows[m] for m in range(MICRO)]
    for layer in range(LAYERS):
        outs_now = []
        for m in range(MICRO):
            result = one_layer(states[m].astype(jnp.float32), allowed, feat_qkv[layer], feat_out[layer], item_query[layer], item_out[layer], gains[layer], train_cache[layer])
            outs_now.append(result)
        states = outs_now
        per_layer.append(jnp.stack(outs_now, axis=0))
    return jnp.stack(per_layer, axis=0)
```

```python
import functools

import jax
import jax.numpy as jnp
from jax import lax
from jax.experimental import pallas as pl
from jax.experimental.pallas import tpu as pltpu
from jax.sharding import PartitionSpec as P

HEADS = 8
NEG = -1e30
VMEM = pltpu.MemorySpace.VMEM


def whole():
    return pl.BlockSpec(memory_space=VMEM)


def prep_kernel(half, x_ref, own_ref, send_ref, wide):
    micro, _, group_dev, _ = x_ref.shape
    feat = lax.axis_index("feat")
    for m in range(micro):
        for part, out in ((feat, own_ref), (1 - feat, send_ref)):
            for r in range(half):
                row = x_ref[m, part * half + r].astype(jnp.float32)
                wide[r * group_dev:(r + 1) * group_dev, :] = row
            out[m] = wide[...].astype(jnp.bfloat16)


def prep_cache_kernel(c_ref, out_ref, wide):
    _, _, rows, group_dev, _ = c_ref.shape
    for kv in range(2):
        for n in range(rows):
            wide[n * group_dev:(n + 1) * group_dev, :] = c_ref[0, kv, n].astype(jnp.float32)
        out_ref[kv] = wide[...].astype(jnp.bfloat16)


def group_of(index, dim, own_count, group_dev, feat, shape):
    at = lax.broadcasted_iota(jnp.int32, shape, dim)
    side = jnp.where(at < own_count, feat, 1 - feat)
    return side * group_dev + lax.rem(at, group_dev)


def norm(x, gain):
    mean_sq = jnp.mean(x * x, axis=-1, keepdims=True)
    return x * lax.rsqrt(mean_sq + 1e-06) * gain


def attend(query, keys, values, masked, low):
    tokens, width = query.shape
    lanes = 128
    key_n = keys.shape[0]
    ones = jnp.ones((key_n, lanes), jnp.bfloat16)
    zero = jnp.zeros((), jnp.bfloat16)
    outs = []
    for pair in range(width // lanes):
        span = slice(pair * lanes, (pair + 1) * lanes)
        q = query[:, span]
        stacked = jnp.concatenate([jnp.where(low, q, zero), jnp.where(low, zero, q)], axis=0)
        scores = lax.dot_general(stacked, keys[:, span], (((1,), (1,)), ((), ())), preferred_element_type=jnp.float32)
        scores = jnp.where(masked, NEG, scores)
        expo = jnp.exp(scores - jnp.max(scores, axis=-1, keepdims=True)).astype(jnp.bfloat16)
        extended = jnp.concatenate([values[:, span], ones], axis=1)
        mixed = jnp.dot(expo, extended, preferred_element_type=jnp.float32)
        mixed = mixed[:, :lanes] / mixed[:, lanes:]
        outs.append(jnp.where(low, mixed[:tokens], mixed[tokens:]).astype(jnp.bfloat16))
    return jnp.concatenate(outs, axis=1)


def layer(h, keys, values, feat_mask, item_mask, wqkv, wout, wquery, witem, gains):
    tokens, width = h.shape
    head_dim = width // HEADS
    scale = 1.0 / head_dim**0.5
    low = lax.rem(lax.broadcasted_iota(jnp.int32, (tokens, 128), 1), 128) < head_dim
    a = norm(h, gains[0:1, :]).astype(jnp.bfloat16)
    qkv = jnp.dot(a, wqkv[...], preferred_element_type=jnp.float32)
    query = (qkv[:, :width].astype(jnp.bfloat16) * scale).astype(jnp.bfloat16)
    rest = qkv[:, width:].astype(jnp.bfloat16)
    mixed = attend(query, rest[:, :width], rest[:, width:], feat_mask, low)
    h1 = h + jnp.dot(mixed, wout[...], preferred_element_type=jnp.float32)
    b = norm(h1, gains[1:2, :]).astype(jnp.bfloat16)
    item_q = jnp.dot(b, wquery[...], preferred_element_type=jnp.float32)
    item_q = (item_q.astype(jnp.bfloat16) * scale).astype(jnp.bfloat16)
    item_mix = attend(item_q, keys, values, item_mask, low)
    return h1 + jnp.dot(item_mix, witem[...], preferred_element_type=jnp.float32)


def layer_kernel(phase, pieces, group_dev, *refs):
    first, second, previous = refs[:3]
    near, far = refs[3:3 + pieces], refs[3 + pieces:3 + 2 * pieces]
    pattern, wqkv, wout, wquery, witem, gains, out_ref = refs[3 + 2 * pieces:]
    section = lax.axis_index("section")
    feat = lax.axis_index("feat")
    tokens = out_ref.shape[0]
    half = tokens // 2
    groups = 2 * group_dev

    @pl.when(section == phase)
    def _():
        if phase == 0:
            h = jnp.concatenate([first[...], second[...]], axis=0).astype(jnp.float32)
        else:
            h = first[...].astype(jnp.float32)
        keys = jnp.concatenate([r[0] for r in near] + [r[0] for r in far], axis=0)
        values = jnp.concatenate([r[1] for r in near] + [r[1] for r in far], axis=0)
        key_n = keys.shape[0]
        eye = group_of(None, 0, half, group_dev, feat, (tokens, groups)) == lax.broadcasted_iota(jnp.int32, (tokens, groups), 1)
        one_hot = eye.astype(jnp.float32)
        table = (pattern[...] != 0).astype(jnp.float32)
        spread = jnp.dot(one_hot, table, preferred_element_type=jnp.float32)
        full = lax.dot_general(spread, one_hot, (((1,), (1,)), ((), ())), preferred_element_type=jnp.float32)
        at_i = lax.broadcasted_iota(jnp.int32, (tokens, tokens), 0)
        at_j = lax.broadcasted_iota(jnp.int32, (tokens, tokens), 1)
        same_row = lax.rem(at_i, half) // group_dev == lax.rem(at_j, half) // group_dev
        allowed = (same_row & (full > 0.5)) | (at_i == at_j)
        feat_mask = jnp.concatenate([~allowed, ~allowed], axis=0)
        item_shape = (tokens, key_n)
        other = group_of(None, 0, half, group_dev, feat, item_shape) != group_of(
            None, 1, key_n // 2, group_dev, feat, item_shape
        )
        item_mask = jnp.concatenate([other, other], axis=0)
        out = layer(h, keys, values, feat_mask, item_mask, wqkv.at[0], wout.at[0], wquery.at[0], witem.at[0], gains.at[0])
        out_ref[...] = out.astype(jnp.bfloat16)

    if phase > 0:

        @pl.when(section != phase)
        def _():
            out_ref[...] = previous[...]


def final_kernel(half, recv_ref, *refs):
    own_refs, out_ref, wide = refs[:-2], refs[-2], refs[-1]
    micro, _, group_dev, _ = out_ref.shape
    feat = lax.axis_index("feat")
    tokens = half * group_dev
    for m in range(micro):
        for part, value in ((feat, own_refs[m][:tokens]), (1 - feat, recv_ref[m])):
            wide[...] = value.astype(jnp.float32)
            for r in range(half):
                out_ref[m, part * half + r] = wide[r * group_dev:(r + 1) * group_dev, :].astype(jnp.bfloat16)


def per_device(test_rows, train_cache, pattern, feat_qkv, feat_out, item_query, item_out, gains):
    micro, test_n, group_dev, width = test_rows.shape
    sections = lax.axis_size("section")
    rows = lax.axis_size("rows")
    half = test_n // 2
    tokens = half * group_dev
    bf16 = jnp.bfloat16
    swap = [(0, 1), (1, 0)]
    own, send = pl.pallas_call(
        functools.partial(prep_kernel, half),
        out_shape=[jax.ShapeDtypeStruct((micro, tokens, width), bf16)] * 2,
        in_specs=[whole()],
        out_specs=[whole()] * 2,
        scratch_shapes=[pltpu.VMEM((tokens, width), jnp.float32)],
        name="prep_rows",
    )(test_rows)
    other = lax.ppermute(send, "feat", swap)
    count = train_cache.shape[2] * group_dev
    cache = pl.pallas_call(
        prep_cache_kernel,
        out_shape=jax.ShapeDtypeStruct((2, count, width), bf16),
        in_specs=[whole()],
        out_specs=whole(),
        scratch_shapes=[pltpu.VMEM((count, width), jnp.float32)],
        name="prep_cache",
    )(train_cache)
    near = [cache]
    for shift in range(1, rows):
        near.append(lax.ppermute(cache, "rows", [(i, (i + shift) % rows) for i in range(rows)]))
    far = [lax.ppermute(piece, "feat", swap) for piece in near]
    weights = (pattern, feat_qkv, feat_out, item_query, item_out, gains)
    results = [None] * micro
    arriving = [None] * micro
    for phase in range(sections):
        for m in range(micro):
            if phase == 0:
                first, second, previous = own[m], other[m], own[m]
            else:
                first, second, previous = arriving[m], arriving[m], results[m]
            operands = (first, second, previous, *near, *far, *weights)
            results[m] = pl.pallas_call(
                functools.partial(layer_kernel, phase, len(near), group_dev),
                out_shape=jax.ShapeDtypeStruct((2 * tokens, width), bf16),
                in_specs=[whole()] * len(operands),
                out_specs=whole(),
                name=f"layer_{phase}_{m}",
                compiler_params=pltpu.CompilerParams(vmem_limit_bytes=32 * 1024 * 1024),
            )(*operands)
            if phase + 1 < sections:
                arriving[m] = lax.ppermute(results[m], "section", [(phase, phase + 1)])
    leaving = jnp.stack([r[tokens:] for r in results])
    entering = lax.ppermute(leaving, "feat", swap)
    out = pl.pallas_call(
        functools.partial(final_kernel, half),
        out_shape=jax.ShapeDtypeStruct((micro, test_n, group_dev, width), bf16),
        in_specs=[whole()] * (1 + micro),
        out_specs=whole(),
        scratch_shapes=[pltpu.VMEM((tokens, width), jnp.float32)],
        name="assemble",
    )(entering, *results)
    return out[None]


def solution(mesh):
    return jax.shard_map(
        per_device,
        mesh=mesh,
        in_specs=(
            P(None, ("groups", "rows"), "feat", None),
            P("section", None, ("groups", "rows"), "feat", None),
            P(),
            P("section", None, None),
            P("section", None, None),
            P("section", None, None),
            P("section", None, None),
            P("section", None, None),
        ),
        out_specs=P("section", None, ("groups", "rows"), "feat", None),
        check_vma=False,
    )
```

```python
import functools

import jax
import jax.numpy as jnp
from jax import lax
from jax.experimental import pallas as pl
from jax.experimental.pallas import tpu as pltpu
from jax.sharding import PartitionSpec as P

HEADS = 8
NEG = -1e30
VMEM = pltpu.MemorySpace.VMEM
GRANT = 12 * 1024 * 1024
LANES = 128


def whole():
    return pl.BlockSpec(memory_space=VMEM)


def call(kernel, outs, operands, name, scratch=(), flops=0, out_specs=None):
    return pl.pallas_call(
        kernel,
        out_shape=outs,
        in_specs=[whole()] * len(operands),
        out_specs=jax.tree.map(lambda _: whole(), outs) if out_specs is None else out_specs,
        scratch_shapes=scratch,
        name=name,
        compiler_params=pltpu.CompilerParams(vmem_limit_bytes=GRANT),
        cost_estimate=pl.CostEstimate(flops=flops, bytes_accessed=1 << 20, transcendentals=0),
    )(*operands)


def group_of(dim, own_count, group_dev, feat, shape):
    at = lax.broadcasted_iota(jnp.int32, shape, dim)
    side = jnp.where(at < own_count, feat, 1 - feat)
    return side * group_dev + lax.rem(at, group_dev)


def norm(x, gain):
    mean_sq = jnp.mean(x * x, axis=-1, keepdims=True)
    return x * lax.rsqrt(mean_sq + 1e-06) * gain


def low_lanes(tokens, head_dim):
    return lax.broadcasted_iota(jnp.int32, (tokens, LANES), 1) < head_dim


def attend(query, keys, values, bias, low):
    tokens, width = query.shape
    key_n = keys.shape[0]
    bias = jnp.concatenate([bias, bias], axis=0)
    ones = jnp.ones((key_n, LANES), jnp.bfloat16)
    zero = jnp.zeros((), jnp.bfloat16)
    outs = []
    for pair in range(width // LANES):
        span = slice(pair * LANES, (pair + 1) * LANES)
        q = query[:, span]
        stacked = jnp.concatenate([jnp.where(low, q, zero), jnp.where(low, zero, q)], axis=0)
        scores = lax.dot_general(stacked, keys[:, span], (((1,), (1,)), ((), ())), preferred_element_type=jnp.float32)
        scores = scores + bias
        expo = jnp.exp(scores - jnp.max(scores, axis=-1, keepdims=True)).astype(jnp.bfloat16)
        extended = jnp.concatenate([values[:, span], ones], axis=1)
        mixed = jnp.dot(expo, extended, preferred_element_type=jnp.float32)
        mixed = mixed[:, :LANES] / mixed[:, LANES:]
        outs.append(jnp.where(low, mixed[:tokens], mixed[tokens:]).astype(jnp.bfloat16))
    return jnp.concatenate(outs, axis=1)


def column_part(h, bias, wqkv, wout, wquery, gains):
    tokens, width = h.shape
    head_dim = width // HEADS
    scale = 1.0 / head_dim**0.5
    a = norm(h, gains[0, 0:1, :]).astype(jnp.bfloat16)
    qkv = jnp.dot(a, wqkv[0], preferred_element_type=jnp.float32)
    query = (qkv[:, :width].astype(jnp.bfloat16) * scale).astype(jnp.bfloat16)
    rest = qkv[:, width:].astype(jnp.bfloat16)
    mixed = attend(query, rest[:, :width], rest[:, width:], bias[...], low_lanes(tokens, head_dim))
    h1 = h + jnp.dot(mixed, wout[0], preferred_element_type=jnp.float32)
    b = norm(h1, gains[0, 1:2, :]).astype(jnp.bfloat16)
    item_q = jnp.dot(b, wquery[0], preferred_element_type=jnp.float32)
    return h1, (item_q.astype(jnp.bfloat16) * scale).astype(jnp.bfloat16)


def item_part(h1, item_q, near, far, bias, witem):
    tokens, width = h1.shape
    keys = jnp.concatenate([near[0], far[0]], axis=0)
    values = jnp.concatenate([near[1], far[1]], axis=0)
    item_mix = attend(item_q, keys, values, bias[...], low_lanes(tokens, width // HEADS))
    return (h1 + jnp.dot(item_mix, witem[0], preferred_element_type=jnp.float32)).astype(jnp.bfloat16)


def to_dense(wide, slabs, group_dev):
    for at, slab in enumerate(slabs):
        wide[at * group_dev:(at + 1) * group_dev, :] = slab.astype(jnp.float32)
    return wide[...].astype(jnp.bfloat16)


def load_kernel(count, x_hbm, cache_hbm, pattern_hbm, *refs):
    weights, outs = refs[:count], refs[count:2 * count]
    own_ref, cache_ref, feat_bias, item_bias, x_vmem, pattern, wide, sems = refs[2 * count:]
    micro, half, group_dev, _ = x_vmem.shape
    feat = lax.axis_index("feat")
    copies = [
        pltpu.make_async_copy(x_hbm.at[:, pl.ds(feat * half, half)], x_vmem, sems.at[0]),
        pltpu.make_async_copy(pattern_hbm, pattern, sems.at[1]),
        pltpu.make_async_copy(cache_hbm, cache_ref, sems.at[2]),
    ]
    for i, (src, dst) in enumerate(zip(weights, outs)):
        copies.append(pltpu.make_async_copy(src, dst, sems.at[3 + i]))
    for copy in copies:
        copy.start()
    copies[0].wait()
    for m in range(micro):
        own_ref[m] = to_dense(wide, [x_vmem[m, r] for r in range(half)], group_dev)
    tokens = feat_bias.shape[0]
    key_n = item_bias.shape[1]
    groups = 2 * group_dev
    copies[1].wait()
    shape = (tokens, groups)
    mine = group_of(0, tokens // 2, group_dev, feat, shape)
    one_hot = (mine == lax.broadcasted_iota(jnp.int32, shape, 1)).astype(jnp.float32)
    table = (pattern[...] != 0).astype(jnp.float32)
    spread = jnp.dot(one_hot, table, preferred_element_type=jnp.float32)
    full = lax.dot_general(spread, one_hot, (((1,), (1,)), ((), ())), preferred_element_type=jnp.float32)
    at_i = lax.broadcasted_iota(jnp.int32, (tokens, tokens), 0)
    at_j = lax.broadcasted_iota(jnp.int32, (tokens, tokens), 1)
    same_row = lax.rem(at_i, tokens // 2) // group_dev == lax.rem(at_j, tokens // 2) // group_dev
    feat_bias[...] = jnp.where((same_row & (full > 0.5)) | (at_i == at_j), 0.0, NEG)
    shape = (tokens, key_n)
    same = group_of(0, tokens // 2, group_dev, feat, shape) == group_of(1, key_n // 2, group_dev, feat, shape)
    item_bias[...] = jnp.where(same, 0.0, NEG)
    for copy in copies[2:]:
        copy.wait()


def enter_kernel(m, own_ref, other_ref, bias, wqkv, wout, wquery, gains, *refs):
    h1_ref, query_ref, wide = refs[-3:]
    _, test_n, group_dev, _ = other_ref.shape
    half = test_n // 2
    feat = lax.axis_index("feat")

    @pl.when(lax.axis_index("section") == 0)
    def _():
        theirs = to_dense(wide, [other_ref[m, feat * half + r] for r in range(half)], group_dev)
        h = jnp.concatenate([own_ref[m], theirs], axis=0).astype(jnp.float32)
        h1_ref[...], query_ref[...] = column_part(h, bias, wqkv, wout, wquery, gains)


def leave_kernel(h1_ref, query_ref, near, far, bias, witem, *refs):
    out_ref = refs[-1]

    @pl.when(lax.axis_index("section") == 0)
    def _():
        out_ref[...] = item_part(h1_ref[...], query_ref[...], near, far, bias, witem)


def layer_kernel(phase, h_ref, prev_ref, near, far, feat_bias, item_bias, wqkv, wout, wquery, witem, gains, out_ref):
    section = lax.axis_index("section")

    @pl.when(section == phase)
    def _():
        h1, query = column_part(h_ref[...].astype(jnp.float32), feat_bias, wqkv, wout, wquery, gains)
        out_ref[...] = item_part(h1, query, near, far, item_bias, witem)

    @pl.when(section != phase)
    def _():
        out_ref[...] = prev_ref[...]


def merge_kernel(count, *refs):
    pieces, out_ref, wide = refs[:count], refs[-2], refs[-1]
    _, _, rows, group_dev, _ = pieces[0].shape
    for kv in range(2):
        out_ref[kv] = to_dense(wide, [piece[0, kv, n] for piece in pieces for n in range(rows)], group_dev)


def from_dense(wide, value, put, group_dev):
    wide[...] = value.astype(jnp.float32)
    for r in range(wide.shape[0] // group_dev):
        put(r, wide[r * group_dev:(r + 1) * group_dev, :].astype(jnp.bfloat16))


def most_kernel(micro, *refs):
    own_refs, recv_refs = refs[:micro], refs[micro:2 * micro - 1]
    out_hbm, out, wide, sems = refs[-4:]
    _, test_n, group_dev, _ = out.shape
    half = test_n // 2
    feat = lax.axis_index("feat")
    copies = []
    for m in range(micro):
        parts = [(feat, own_refs[m][:half * group_dev])]
        if m + 1 < micro:
            parts.append((1 - feat, recv_refs[m][...]))
        for part, value in parts:
            def put(r, slab):
                out[m, part * half + r] = slab

            from_dense(wide, value, put, group_dev)
        where = m if m + 1 < micro else (m, pl.ds(feat * half, half))
        copies.append(pltpu.make_async_copy(out.at[where], out_hbm.at[where], sems.at[m]))
        copies[-1].start()
    for copy in copies:
        copy.wait()


def last_kernel(recv_ref, _, out_hbm, out, wide, sem):
    micro, test_n, group_dev, _ = out_hbm.shape
    half = test_n // 2

    def put(r, slab):
        out[r] = slab

    from_dense(wide, recv_ref[...], put, group_dev)
    start = (1 - lax.axis_index("feat")) * half
    copy = pltpu.make_async_copy(out, out_hbm.at[micro - 1, pl.ds(start, half)], sem)
    copy.start()
    copy.wait()


def per_device(test_rows, train_cache, pattern, feat_qkv, feat_out, item_query, item_out, gains):
    micro, test_n, group_dev, width = test_rows.shape
    sections = lax.axis_size("section")
    rows = lax.axis_size("rows")
    half = test_n // 2
    tokens = test_n * group_dev
    bf16, f32 = jnp.bfloat16, jnp.float32
    shaped = jax.ShapeDtypeStruct
    swap = [(0, 1), (1, 0)]
    other = lax.ppermute(test_rows, "feat", swap)
    pieces = []
    for shift in range(1, rows):
        pieces.append(lax.ppermute(train_cache, "rows", [(i, (i + shift) % rows) for i in range(rows)]))
    count = train_cache.shape[2] * group_dev * rows
    weights = (feat_qkv, feat_out, item_query, item_out, gains)
    *weights, own, cache, feat_bias, item_bias = pl.pallas_call(
        functools.partial(load_kernel, len(weights)),
        out_shape=[shaped(w.shape, w.dtype) for w in weights] + [
            shaped((micro, tokens // 2, width), bf16),
            shaped(train_cache.shape, bf16),
            shaped((tokens, tokens), f32),
            shaped((tokens, 2 * count), f32),
        ],
        in_specs=[pl.BlockSpec(memory_space=pltpu.MemorySpace.HBM)] * (3 + len(weights)),
        out_specs=[whole()] * (4 + len(weights)),
        scratch_shapes=[
            pltpu.VMEM((micro, half, group_dev, width), bf16),
            pltpu.VMEM(pattern.shape, pattern.dtype),
            pltpu.VMEM((tokens // 2, width), f32),
            pltpu.SemaphoreType.DMA((3 + len(weights),)),
        ],
        name="load",
        compiler_params=pltpu.CompilerParams(vmem_limit_bytes=GRANT),
    )(*[pltpu.with_memory_space_constraint(v, pltpu.MemorySpace.HBM) for v in (test_rows, train_cache, pattern, *weights)])
    wqkv, wout, wquery, witem, gains = weights
    dense = 2 * tokens * width * width
    block = shaped((tokens, width), bf16)

    def enter(m, *after):
        return call(
            functools.partial(enter_kernel, m), (shaped((tokens, width), f32), block),
            (own, other, feat_bias, wqkv, wout, wquery, gains, *after), f"enter_{m}",
            scratch=[pltpu.VMEM((tokens // 2, width), f32)], flops=5 * dense,
        )

    begun = [enter(0)]
    near = call(
        functools.partial(merge_kernel, rows), shaped((2, count, width), bf16), (cache, *pieces, begun[0][1]), "merge",
        scratch=[pltpu.VMEM((count, width), f32)],
    )
    far = lax.ppermute(near, "feat", swap)
    begun.append(enter(1, near))
    results, arriving = [], []
    for m in range(micro):
        if m >= len(begun):
            begun.append(enter(m, results[-1]))
        operands = (*begun[m], near, far, item_bias, witem, begun[-1][1])
        results.append(call(leave_kernel, block, operands, f"leave_{m}", flops=dense))
        arriving.append(lax.ppermute(results[m], "section", [(0, 1)]))
    for phase in range(1, sections):
        for m in range(micro):
            operands = (arriving[m], results[m], near, far, feat_bias, item_bias, wqkv, wout, wquery, witem, gains)
            results[m] = call(functools.partial(layer_kernel, phase), block, operands, f"layer_{phase}_{m}", flops=6 * dense)
            if phase + 1 < sections:
                arriving[m] = lax.ppermute(results[m], "section", [(phase, phase + 1)])
    received = [lax.ppermute(r[tokens // 2:], "feat", swap) for r in results]
    out_shape = shaped((micro, test_n, group_dev, width), bf16)
    hbm = pl.BlockSpec(memory_space=pl.ANY)
    out = call(
        functools.partial(most_kernel, micro), out_shape, (*results, *received[:-1]), "most", out_specs=hbm,
        scratch=[
            pltpu.VMEM(out_shape.shape, bf16), pltpu.VMEM((tokens // 2, width), f32), pltpu.SemaphoreType.DMA((micro,)),
        ],
    )
    out = pl.pallas_call(
        last_kernel,
        out_shape=out_shape,
        in_specs=[whole(), hbm],
        out_specs=hbm,
        input_output_aliases={1: 0},
        scratch_shapes=[
            pltpu.VMEM((half, group_dev, width), bf16), pltpu.VMEM((tokens // 2, width), f32), pltpu.SemaphoreType.DMA,
        ],
        name="last",
        compiler_params=pltpu.CompilerParams(vmem_limit_bytes=GRANT),
    )(received[-1], out)
    return out[None]


def solution(mesh):
    return jax.shard_map(
        per_device,
        mesh=mesh,
        in_specs=(
            P(None, ("groups", "rows"), "feat", None),
            P("section", None, ("groups", "rows"), "feat", None),
            P(),
            P("section", None, None),
            P("section", None, None),
            P("section", None, None),
            P("section", None, None),
            P("section", None, None),
        ),
        out_specs=P("section", None, ("groups", "rows"), "feat", None),
        check_vma=False,
    )
```
